1024 devices in a mesh: expert: 32 (over z, x_hi), dp: 32 (over y, x_lo, core).
Axes of the slice: x: 8 (x_hi: 4, x_lo: 2; x = x_hi * 2 + x_lo), y: 8, z: 8, core: 2. Of those that a mesh axis runs over, the one named last changes fastest.
Arguments:
- tokens: bfloat16 [8192, 64, 384], P(('expert', 'dp')), may hold values from -6 to 6
- router: bfloat16 [384, 32], replicated, may hold values from -8.675276 to 8.675276
- w_in: bfloat16 [32, 384, 1536], P('expert'), may hold values from -0.3125 to 0.3125
- w_out: bfloat16 [32, 384, 1536], P('expert'), may hold values from -0.15625 to 0.15625
- out_grad: bfloat16 [8192, 64, 384], P(('expert', 'dp')), may hold values from -6 to 6
Outputs:
- tokens_grad: bfloat16 [8192, 64, 384], P(('expert', 'dp'))
- w_in_grad: float32 [32, 384, 1536], P('expert', 'dp')
- w_out_grad: float32 [32, 384, 1536], P('expert', 'dp')
- router_grad: float32 [384, 32], P('dp')
The draws below stay inside these ranges and needn't reach their ends.
All inputs are finite; a program needn't handle non-finite values.
Results may differ from the reference program's by a relative error of at most 0.029.
Values may be sent and summed in bfloat16 or wider, within the bound.
A program may use at most 64 MiB of HBM per device.

```python
import math
import jax
import jax.numpy as jnp
from jax import lax

D = 384
FF = 1536
M = 64
IMG_DEV = 8
EXPERTS = 32
IMAGES = 8192
N_EXPERT = 32
N_DP = 32


def draw_router(key, part):
    keys = jax.random.split(jax.random.fold_in(key, 11), 1)
    return (jnp.clip(jax.random.normal(keys[0], (D, EXPERTS), jnp.float32), -4.0, 4.0) * (3.0 / math.sqrt(D))).astype(jnp.bfloat16)


def levels(key, dims, cuts, low, high):
    level = 1.0
    for axis_at, parts in cuts:
        steps = jax.random.uniform(jax.random.fold_in(jax.random.fold_in(key, 6), axis_at), (parts,), jnp.float32, low / len(cuts), high / len(cuts))
        level = level * jnp.repeat(jnp.exp(steps), dims[axis_at] // parts).reshape((-1,) + (1,) * (len(dims) - 1 - axis_at))
    return level


def bell_draw(stream_key, dims, deviation, most, pieces=(), held_as=jnp.bfloat16):
    factor_of = levels(stream_key, dims, pieces, -0.22, 0.18) if pieces else 1.0
    values = jax.random.normal(stream_key, dims, jnp.float32) * deviation * factor_of
    return jnp.minimum(jnp.maximum(values, -most), most).astype(held_as)


def setup_inputs(seed: int = 0) -> dict:
    key_of = jax.random.split(jax.random.key(seed), 6)
    return {
        "tokens": bell_draw(key_of[0], (IMAGES, M, D), 1.0, 6.0, ((0, 1024),)),
        "router": draw_router(jax.random.fold_in(key_of[5], 71), 0),
        "w_in": bell_draw(key_of[2], (EXPERTS, D, FF), D ** -0.5, 0.3125, ((0, 32),)),
        "w_out": bell_draw(key_of[3], (EXPERTS, D, FF), FF ** -0.5, 0.15625, ((0, 32),)),
        "out_grad": bell_draw(key_of[4], (IMAGES, M, D), 1.0, 6.0, ((0, 1024),)),
    }


def gelu_pair(value):
    coef = math.sqrt(2.0 / math.pi)
    inner = coef * (value + 0.044715 * value * value * value)
    tangent = jnp.tanh(inner)
    result = 0.5 * value * (1.0 + tangent)
    slope = 0.5 * (1.0 + tangent) + 0.5 * value * (1.0 - tangent * tangent) * coef * (1.0 + 3.0 * 0.044715 * value * value)
    return (result, slope)

def round_keep(value):
    return lax.optimization_barrier(value.astype(jnp.bfloat16)).astype(jnp.float32)

def reference(tokens, router, w_in, w_out, out_grad):
    f32 = jnp.float32
    bf16 = jnp.bfloat16
    grouped = tokens.reshape(N_EXPERT, N_DP, IMG_DEV, M, D).transpose(1, 0, 2, 3, 4).reshape(N_DP, N_EXPERT * IMG_DEV, M, D)
    grads_in = out_grad.reshape(N_EXPERT, N_DP, IMG_DEV, M, D).transpose(1, 0, 2, 3, 4).reshape(N_DP, N_EXPERT * IMG_DEV, M, D)
    router_f = router.astype(f32)
    w_in_f = w_in.astype(f32)
    w_out_f = w_out.astype(f32)

    def group(carry, item):
        win_acc, wout_acc, router_acc = carry
        toks, cotan = item
        toks_f = toks.astype(f32)
        logits = jnp.einsum('bmd,de->bme', toks_f, router_f)
        dispatch = jax.nn.softmax(logits, axis=1)
        combine = jax.nn.softmax(logits, axis=2)
        dispatch_b = dispatch.astype(bf16).astype(f32)
        combine_b = combine.astype(bf16).astype(f32)
        slot_in = jnp.einsum('bme,bmd->bed', dispatch_b, toks_f).astype(bf16).astype(f32)
        slot_grad = jnp.einsum('bme,bmd->bed', combine_b, cotan.astype(f32)).astype(bf16).astype(f32)
        pre_act = jnp.einsum('bed,edf->bef', slot_in, w_in_f)
        value, slope = gelu_pair(pre_act)
        hidden = value.astype(bf16).astype(f32)
        slot_out = jnp.einsum('bef,edf->bed', hidden, w_out_f).astype(bf16).astype(f32)
        hid_grad = jnp.einsum('bed,edf->bef', slot_grad, w_out_f)
        pre_grad = (hid_grad * slope).astype(bf16).astype(f32)
        slot_in_grad = jnp.einsum('bef,edf->bed', pre_grad, w_in_f).astype(bf16).astype(f32)
        win_part = round_keep(jnp.einsum('bed,bef->edf', slot_in, pre_grad))
        wout_part = round_keep(jnp.einsum('bed,bef->edf', slot_grad, hidden))
        comb_grad = jnp.einsum('bmd,bed->bme', cotan.astype(f32), slot_out)
        disp_grad = jnp.einsum('bmd,bed->bme', toks_f, slot_in_grad)
        logit_grad = combine * (comb_grad - lax.optimization_barrier(jnp.sum(combine * comb_grad, axis=2, keepdims=True)))
        logit_grad = logit_grad + dispatch * (disp_grad - lax.optimization_barrier(jnp.sum(dispatch * disp_grad, axis=1, keepdims=True)))
        logit_grad = logit_grad.astype(bf16).astype(f32)
        tok_grad = jnp.einsum('bme,bed->bmd', dispatch_b, slot_in_grad) + jnp.einsum('bme,de->bmd', logit_grad, router_f)
        router_part = jnp.einsum('bmd,bme->de', toks_f, logit_grad)
        return ((win_acc + win_part, wout_acc + wout_part, router_acc + router_part), tok_grad.astype(bf16))
    init = (jnp.zeros((EXPERTS, D, FF), f32), jnp.zeros((EXPERTS, D, FF), f32), jnp.zeros((D, EXPERTS), f32))
    (win_grad, wout_grad, router_grad), stacked = lax.scan(group, init, (grouped, grads_in))
    tokens_grad = stacked.reshape(N_DP, N_EXPERT, IMG_DEV, M, D).transpose(1, 0, 2, 3, 4).reshape(IMAGES, M, D)
    return (tokens_grad, win_grad, wout_grad, router_grad)
```

```python
import functools
import math

import jax
import jax.numpy as jnp
from jax import lax
from jax.experimental import pallas as pl
from jax.experimental.pallas import tpu as pltpu
from jax.sharding import PartitionSpec as P

MESH = pl.DeviceIdType.MESH
F32 = jnp.float32
BF16 = jnp.bfloat16

D = 384
FF = 1536
M = 64
IMG = 8
TOK = IMG * M
NE = 32
NDP = 32
NY = 8
RING = D // NY
ROWS = D // NDP
SLOTS = NE * IMG
CHUNK = 512
NN = (((1,), (0,)), ((), ()))
NT = (((1,), (1,)), ((), ()))
TN = (((0,), (0,)), ((), ()))


def dot(a, b, dims):
    return lax.dot_general(a, b, dims, preferred_element_type=F32)


def iota(shape, axis):
    return lax.broadcasted_iota(jnp.int32, shape, axis)


def mask01(condition):
    return jnp.where(condition, 1.0, 0.0).astype(BF16)


def gelu_pair(value):
    coef = math.sqrt(2.0 / math.pi)
    inner = coef * (value + 0.044715 * value * value * value)
    tangent = jnp.tanh(inner)
    result = 0.5 * value * (1.0 + tangent)
    slope = 0.5 * (1.0 + tangent) + 0.5 * value * (1.0 - tangent * tangent) * coef * (
        1.0 + 3.0 * 0.044715 * value * value
    )
    return (result, slope)


def by_image(reduce, fill, value, low):
    first = reduce(jnp.where(low, value, fill), axis=1, keepdims=True)
    second = reduce(jnp.where(low, fill, value), axis=1, keepdims=True)
    return jnp.where(low, first, second)


def kernel(
    tok_hbm,
    og_hbm,
    router_ref,
    win_hbm,
    wout_hbm,
    tok_out,
    dw_out,
    router_out,
    tok,
    og,
    win,
    wout,
    slots_out,
    slots_in,
    back_out,
    back_in,
    act,
    slope,
    disp,
    comb,
    place,
    tok_perm,
    mine,
    theirs,
    partner,
    ring_out,
    ring_in,
    last_out,
    last_in,
    part_out,
    part_in,
    part_sum,
    full_in,
    load_sem,
    slot_sem,
    back_sem,
    pair_sem,
    ring_sem,
    last_sem,
    part_sem,
    full_sem,
):
    e = lax.axis_index("expert")
    d = lax.axis_index("dp")
    y = lax.div(d, 4)
    core = lax.rem(d, 2)

    loads = [
        pltpu.make_async_copy(src, dst, load_sem.at[i])
        for i, (src, dst) in enumerate(
            ((tok_hbm, tok), (og_hbm, og), (win_hbm, win), (wout_hbm, wout))
        )
    ]
    for load in loads:
        load.start()

    barrier = pltpu.get_barrier_semaphore()

    def greet(k, carry):
        pl.semaphore_signal(
            barrier, inc=1, device_id=(lax.rem(e + k, NE), d), device_id_type=MESH
        )
        pl.semaphore_signal(
            barrier, inc=1, device_id=(e, lax.rem(d + k, NDP)), device_id_type=MESH
        )
        return carry

    lax.fori_loop(1, NE, greet, 0)

    loads[0].wait()
    logits = dot(router_ref[...], tok[...], NT)
    top = jnp.max(logits, axis=0, keepdims=True)
    raised = jnp.exp(logits - top)
    combine = raised / jnp.sum(raised, axis=0, keepdims=True)
    low = iota((NE, 128), 1) < M
    parts = []
    for j in range(TOK // 128):
        x = logits[:, 128 * j : 128 * (j + 1)]
        raised = jnp.exp(x - by_image(jnp.max, -jnp.inf, x, low))
        parts.append(raised / by_image(jnp.sum, 0.0, raised, low))
    dispatch = jnp.concatenate(parts, axis=1)
    disp[...] = dispatch
    comb[...] = combine

    spread = mask01(iota((SLOTS, NE), 0) // IMG == iota((SLOTS, NE), 1))
    own_image = iota((SLOTS, TOK), 0) % IMG == iota((SLOTS, TOK), 1) // M
    placed = jnp.where(own_image, dot(spread, dispatch.astype(BF16), NN), 0.0).astype(BF16)
    place[...] = placed
    slots_out[0] = dot(placed, tok[...], NN).astype(BF16)
    pl.semaphore_wait(barrier, 2 * (NE - 1))

    def exchange(src, dst, sems):
        def send(k, carry):
            to = lax.rem(e + k, NE)
            pltpu.make_async_remote_copy(
                src_ref=src.at[pl.ds(pl.multiple_of(to * IMG, IMG), IMG)],
                dst_ref=dst.at[pl.ds(pl.multiple_of(e * IMG, IMG), IMG)],
                send_sem=sems.at[0],
                recv_sem=sems.at[1],
                device_id=(to, d),
                device_id_type=MESH,
            ).start()
            return carry

        lax.fori_loop(1, NE, send, 0)
        own = pl.ds(pl.multiple_of(e * IMG, IMG), IMG)
        pltpu.make_async_copy(src.at[own], dst.at[own], sems.at[1]).start()

    def arrived(dst, sems):
        pltpu.make_async_copy(dst, dst, sems.at[1]).wait()

    def sent(src, sems):
        some = src.at[pl.ds(0, (NE - 1) * IMG)]
        pltpu.make_async_copy(some, some, sems.at[0]).wait()

    exchange(slots_out.at[0], slots_in.at[0], slot_sem.at[0])
    loads[1].wait()
    placed = jnp.where(own_image, dot(spread, combine.astype(BF16), NN), 0.0).astype(BF16)
    slots_out[1] = dot(placed, og[...], NN).astype(BF16)
    exchange(slots_out.at[1], slots_in.at[1], slot_sem.at[1])

    for q in range(4):
        row = iota((3 * NDP, D), 0)
        pick = mask01(iota((3 * NDP, D), 1) == ROWS * (row % NDP) + 4 * (row // NDP) + q)
        tok_perm[:, TOK * q : TOK * (q + 1)] = dot(pick, tok[...], NT).astype(BF16)

    loads[2].wait()
    loads[3].wait()
    arrived(slots_in.at[0], slot_sem.at[0])
    total = jnp.zeros((SLOTS, D), F32)
    for c in range(0, FF, CHUNK):
        value, rise = gelu_pair(dot(slots_in[0], win[:, c : c + CHUNK], NN))
        act[1, :, c : c + CHUNK] = value.astype(BF16)
        slope[:, c : c + CHUNK] = rise
        total = total + dot(value.astype(BF16), wout[:, c : c + CHUNK], NT)
    back_out[0] = total.astype(BF16)
    exchange(back_out.at[0], back_in.at[0], back_sem.at[0])

    arrived(slots_in.at[1], slot_sem.at[1])
    total = jnp.zeros((SLOTS, D), F32)
    for c in range(0, FF, CHUNK):
        grad = dot(slots_in[1], wout[:, c : c + CHUNK], NN)
        grad = (grad * slope[:, c : c + CHUNK]).astype(BF16)
        act[0, :, c : c + CHUNK] = grad
        total = total + dot(grad, win[:, c : c + CHUNK], NT)
    back_out[1] = total.astype(BF16)
    exchange(back_out.at[1], back_in.at[1], back_sem.at[1])

    def weight_term(kind, dst):
        for c in range(0, FF, CHUNK):
            dst[:, c : c + CHUNK] = dot(
                slots_in[kind], act[kind, :, c : c + CHUNK], TN
            ).astype(BF16)

    weight_term(1 - core, theirs)
    pair = pltpu.make_async_remote_copy(
        src_ref=theirs,
        dst_ref=partner,
        send_sem=pair_sem.at[0],
        recv_sem=pair_sem.at[1],
        device_id=(e, d + 1 - 2 * core),
        device_id_type=MESH,
    )
    pair.start()
    weight_term(core, mine)

    sign = 1 - 2 * core

    def at_ring(step):
        return lax.rem(y + sign * step + 2 * NY, NY)

    def ring_copy(slot, way):
        to = lax.rem(y + sign * way + NY, NY) * 4 + lax.rem(d, 4)
        return pltpu.make_async_remote_copy(
            src_ref=ring_out.at[slot],
            dst_ref=ring_in.at[slot],
            send_sem=ring_sem.at[0, slot],
            recv_sem=ring_sem.at[1, slot],
            device_id=(e, to),
            device_id_type=MESH,
        )

    long = [ring_copy(t, 1) for t in range(4)]
    short = [ring_copy(4 + t, -1) for t in range(3)]

    def own_part(step):
        rows = pl.ds(pl.multiple_of(at_ring(step) * RING, 16), RING)
        return mine[rows, :].astype(F32) + partner[rows, :].astype(F32)

    def ring_step(t):
        value = own_part(4 - t)
        if t:
            long[t - 1].wait_recv()
            value = value + ring_in[t - 1].astype(F32)
        ring_out[t] = value.astype(BF16)
        long[t].start()
        if t < 3:
            value = own_part(t - 3)
            if t:
                short[t - 1].wait_recv()
                value = value + ring_in[3 + t].astype(F32)
            ring_out[4 + t] = value.astype(BF16)
            short[t].start()

    pair.wait_recv()
    ring_step(0)

    move = mask01(
        (iota((SLOTS, SLOTS), 1) // IMG == iota((SLOTS, SLOTS), 0) % NE)
        & (iota((SLOTS, SLOTS), 1) % IMG == iota((SLOTS, SLOTS), 0) // NE)
    )

    def per_slot(rows, values):
        rows = dot(move, rows, NN).astype(BF16)
        out = []
        for j in range(TOK // 128):
            both = dot(
                rows[2 * NE * j : 2 * NE * (j + 1)], values[128 * j : 128 * (j + 1)], NT
            )
            out.append(jnp.where(low, both[:NE], both[NE:]))
        return out

    arrived(back_in.at[0], back_sem.at[0])
    comb_grad = jnp.concatenate(per_slot(back_in[0], og), axis=1)
    combine = comb[...]
    comb_part = combine * (comb_grad - jnp.sum(combine * comb_grad, axis=0, keepdims=True))

    ring_step(1)

    arrived(back_in.at[1], back_sem.at[1])
    parts = []
    for j, grad in enumerate(per_slot(back_in[1], tok)):
        share = disp[:, 128 * j : 128 * (j + 1)]
        parts.append(share * (grad - by_image(jnp.sum, 0.0, share * grad, low)))
    logit_grad = (comb_part + jnp.concatenate(parts, axis=1)).astype(BF16)

    blank = jnp.zeros((NE, TOK), BF16)
    spots = jnp.concatenate(
        [
            jnp.concatenate([logit_grad if i == q else blank for i in range(4)], axis=1)
            for q in range(4)
        ],
        axis=0,
    )
    mixed = dot(tok_perm[...], spots, NT)
    mixed = jnp.concatenate([mixed[NDP * g : NDP * (g + 1)] for g in range(3)], axis=1)
    for r in range(NDP):
        part_out[r] = mixed[r : r + 1]

    def spread_part(k, carry):
        to = lax.rem(d + k, NDP)
        pltpu.make_async_remote_copy(
            src_ref=part_out.at[to],
            dst_ref=part_in.at[d],
            send_sem=part_sem.at[0],
            recv_sem=part_sem.at[1],
            device_id=(e, to),
            device_id_type=MESH,
        ).start()
        return carry

    lax.fori_loop(1, NDP, spread_part, 0)
    pltpu.make_async_copy(part_out.at[d], part_in.at[d], part_sem.at[1]).start()

    tok_out[...] = (
        dot(place[...], back_in[1], TN) + dot(logit_grad, router_ref[...], TN)
    ).astype(BF16)

    ring_step(2)

    pltpu.make_async_copy(part_in, part_in, part_sem.at[1]).wait()
    part_sum[...] = jnp.sum(part_in[...], axis=0)

    def spread_full(k, carry):
        pltpu.make_async_remote_copy(
            src_ref=part_sum,
            dst_ref=full_in.at[e],
            send_sem=full_sem.at[0],
            recv_sem=full_sem.at[1],
            device_id=(lax.rem(e + k, NE), d),
            device_id_type=MESH,
        ).start()
        return carry

    lax.fori_loop(1, NE, spread_full, 0)
    pltpu.make_async_copy(part_sum, full_in.at[e], full_sem.at[1]).start()

    ring_step(3)

    long[3].wait_recv()
    short[2].wait_recv()
    value = own_part(0) + ring_in[3].astype(F32) + ring_in[6].astype(F32)
    for i in range(4):
        last_out[i] = value[ROWS * i : ROWS * (i + 1)].astype(BF16)
    me = lax.rem(d, 4)

    def last_send(k, carry):
        to = lax.rem(me + k, 4)
        pltpu.make_async_remote_copy(
            src_ref=last_out.at[to],
            dst_ref=last_in.at[me],
            send_sem=last_sem.at[0],
            recv_sem=last_sem.at[1],
            device_id=(e, d - me + to),
            device_id_type=MESH,
        ).start()
        return carry

    lax.fori_loop(1, 4, last_send, 0)
    pltpu.make_async_copy(last_out.at[me], last_in.at[me], last_sem.at[1]).start()

    pltpu.make_async_copy(full_in, full_in, full_sem.at[1]).wait()
    router_out[...] = jnp.sum(full_in[...], axis=0)

    pltpu.make_async_copy(last_in, last_in, last_sem.at[1]).wait()
    dw_out[0] = last_in[0].astype(F32) + last_in[2].astype(F32)
    dw_out[1] = last_in[1].astype(F32) + last_in[3].astype(F32)

    for kind in range(2):
        sent(slots_out.at[kind], slot_sem.at[kind])
        sent(back_out.at[kind], back_sem.at[kind])
    pair.wait_send()
    for copy in long + short:
        copy.wait_send()
    some = last_out.at[pl.ds(0, 3)]
    pltpu.make_async_copy(some, some, last_sem.at[0]).wait()
    some = part_out.at[pl.ds(0, NDP - 1)]
    pltpu.make_async_copy(some, some, part_sem.at[0]).wait()
    some = full_in.at[pl.ds(0, NE - 1)]
    pltpu.make_async_copy(some, some, full_sem.at[0]).wait()


def on_device(tokens, router, w_in, w_out, out_grad):
    vmem = pl.BlockSpec(memory_space=pltpu.VMEM)
    hbm = pl.BlockSpec(memory_space=pl.ANY)
    dma = pltpu.SemaphoreType.DMA
    tok_grad, dw, router_grad = pl.pallas_call(
        kernel,
        out_shape=(
            jax.ShapeDtypeStruct((TOK, D), BF16),
            jax.ShapeDtypeStruct((2, ROWS, FF), F32),
            jax.ShapeDtypeStruct((1, D), F32),
        ),
        in_specs=[hbm, hbm, vmem, hbm, hbm],
        out_specs=[vmem, vmem, vmem],
        scratch_shapes=[
            pltpu.VMEM((TOK, D), BF16),
            pltpu.VMEM((TOK, D), BF16),
            pltpu.VMEM((D, FF), BF16),
            pltpu.VMEM((D, FF), BF16),
            pltpu.VMEM((2, SLOTS, D), BF16),
            pltpu.VMEM((2, SLOTS, D), BF16),
            pltpu.VMEM((2, SLOTS, D), BF16),
            pltpu.VMEM((2, SLOTS, D), BF16),
            pltpu.VMEM((2, SLOTS, FF), BF16),
            pltpu.VMEM((SLOTS, FF), F32),
            pltpu.VMEM((NE, TOK), F32),
            pltpu.VMEM((NE, TOK), F32),
            pltpu.VMEM((SLOTS, TOK), BF16),
            pltpu.VMEM((3 * NDP, 4 * TOK), BF16),
            pltpu.VMEM((D, FF), BF16),
            pltpu.VMEM((D, FF), BF16),
            pltpu.VMEM((D, FF), BF16),
            pltpu.VMEM((7, RING, FF), BF16),
            pltpu.VMEM((7, RING, FF), BF16),
            pltpu.VMEM((4, ROWS, FF), BF16),
            pltpu.VMEM((4, ROWS, FF), BF16),
            pltpu.VMEM((NDP, 1, D), F32),
            pltpu.VMEM((NDP, 1, D), F32),
            pltpu.VMEM((1, D), F32),
            pltpu.VMEM((NE, 1, D), F32),
            dma((4,)),
            dma((2, 2)),
            dma((2, 2)),
            dma((2,)),
            dma((2, 7)),
            dma((2,)),
            dma((2,)),
            dma((2,)),
        ],
        compiler_params=pltpu.CompilerParams(
            collective_id=0, has_side_effects=True, vmem_limit_bytes=48 << 20
        ),
    )(
        tokens.reshape(TOK, D),
        out_grad.reshape(TOK, D),
        router.T,
        w_in.reshape(D, FF),
        w_out.reshape(D, FF),
    )
    return (
        tok_grad.reshape(IMG, M, D),
        dw[0:1],
        dw[1:2],
        router_grad.reshape(ROWS, NE),
    )


def solution(mesh):
    placed = (
        P(("expert", "dp"), None, None),
        P(),
        P("expert", None, None),
        P("expert", None, None),
        P(("expert", "dp"), None, None),
    )
    return jax.shard_map(
        on_device,
        mesh=mesh,
        in_specs=placed,
        out_specs=(
            P(("expert", "dp"), None, None),
            P("expert", "dp", None),
            P("expert", "dp", None),
            P("dp", None),
        ),
        check_vma=False,
    )
```
